32 devices in a mesh: group: 2 (over x), tm: 4 (over y, core), inline: 4 (over z).
Axes of the slice: x: 2, y: 2, z: 4, core: 2. Of those that a mesh axis runs over, the one named last changes fastest.
Arguments:
- near_trace: float32 [128, 512], P(('group', 'inline'), 'tm'), parts along dimension 0, may hold values from -1.5 to 1.5
- far_trace: float32 [128, 512], P(('group', 'inline'), 'tm'), parts along dimension 0, may hold values from -1.5 to 1.5
- inline_weight: int32 [128, 512], P(('group', 'inline'), 'tm'), parts along dimension 0, may hold values from 0 to 15
- time_weight: int32 [128, 512], P(('group', 'inline'), 'tm'), parts along dimension 0, may hold values from 0 to 15
- lag_low: int32 [128], P(('group', 'inline')), parts along dimension 0, may hold values from 0 to 15
- lag_high: int32 [128], P(('group', 'inline')), parts along dimension 0, may hold values from 48 to 63
- strain: int32 [16], P(('group', 'tm')), parts along dimension 0, may hold values from 1 to 3
Outputs:
- accumulated: float32 [64, 128, 512], P(None, ('group', 'inline'), 'tm'), parts along dimension 1
The draws below stay inside these ranges and needn't reach their ends.
There are 2 independent parts, one for each index of `group`. The reference program is written for one: setup_inputs(seed, part) draws one part's arguments, and reference() takes and returns one part's arrays. A program takes and returns all parts, laid end to end along the dimension named above; each array names one. Nothing has to cross between parts.
All inputs are finite; a program needn't handle non-finite values.
Results may differ from the reference program's by a relative error of at most 0.0003.
Values sent between devices are 32-bit elements; how exact they have to be, the bound alone decides.
A program may use at most 64 MiB of HBM per device.

```python
import math
import jax
import jax.numpy as jnp
from jax import lax

L = 64
STRETCH = 64
ITERS = 10
NTR = 64
NS = 512
NCHUNK = 8


def survey_pair(key):
    subkeys = jax.random.split(jax.random.fold_in(key, 7321), 6)
    period = jax.random.uniform(subkeys[0], (NTR, 1), jnp.float32, 12.0, 20.0)
    phase_shift = jax.random.uniform(subkeys[1], (NTR, 1), jnp.float32, 0.0, 1.0)
    delay_lags = jax.random.uniform(subkeys[2], (NTR, 1), jnp.float32, 0.0, 16.0)
    samples = jnp.arange(NS, dtype=jnp.float32)[None, :]
    amplitude = jax.random.uniform(subkeys[3], (NTR, 1), jnp.float32, 0.7, 1.3)
    near_noise = 0.06 * jax.random.truncated_normal(subkeys[4], -3.0, 3.0, (NTR, NS), jnp.float32)
    far_noise = 0.06 * jax.random.truncated_normal(subkeys[5], -3.0, 3.0, (NTR, NS), jnp.float32)
    near_angle = 2.0 * math.pi * (jnp.mod(samples, period) / period + phase_shift)
    far_angle = 2.0 * math.pi * (jnp.mod(samples - delay_lags, period) / period + phase_shift)
    near_values = amplitude * jnp.cos(near_angle) + near_noise
    far_values = amplitude * jnp.cos(far_angle) + far_noise
    return (jnp.clip(near_values, -1.5, 1.5), jnp.clip(far_values, -1.5, 1.5))


def draw_near_trace(key, part):
    return survey_pair(key)[0].astype(jnp.float32)


def draw_far_trace(key, part):
    return survey_pair(key)[1].astype(jnp.float32)


def place_ends(values, own_key, least, top_value):
    spot = [jax.random.randint(jax.random.fold_in(own_key, axis), (), 0, length) for axis, length in enumerate(values.shape)]
    longest = values.shape.index(max(values.shape))
    neighbour = spot[:longest] + [(spot[longest] + 1) % values.shape[longest]] + spot[longest + 1:]
    return values.at[tuple(spot)].set(least).at[tuple(neighbour)].set(top_value)


def setup_inputs(seed: int = 0, part: int = 0) -> dict:
    seeds = jax.random.split(jax.random.key(seed), 8)
    own_keys = jax.random.split(jax.random.fold_in(seeds[7], part), 8)
    near_trace = draw_near_trace(jax.random.fold_in(jax.random.fold_in(seeds[7], part), 71), part)
    far_trace = draw_far_trace(jax.random.fold_in(jax.random.fold_in(seeds[7], part), 71), part)
    inline_weight = place_ends(jax.random.randint(own_keys[2], (NTR, NS), 0, 16), jax.random.fold_in(own_keys[2], 1), 0, 15).astype(jnp.int32)
    time_weight = place_ends(jax.random.randint(own_keys[3], (NTR, NS), 0, 16), jax.random.fold_in(own_keys[3], 1), 0, 15).astype(jnp.int32)
    lag_low = place_ends(jax.random.randint(own_keys[4], (NTR,), 0, 16), jax.random.fold_in(own_keys[4], 1), 0, 15).astype(jnp.int32)
    lag_high = place_ends(jax.random.randint(own_keys[5], (NTR,), 48, 64), jax.random.fold_in(own_keys[5], 1), 48, 63).astype(jnp.int32)
    strain = place_ends(jax.random.randint(own_keys[6], (NCHUNK,), 1, 4), jax.random.fold_in(own_keys[6], 1), 1, 3).astype(jnp.int32)
    return dict(near_trace=near_trace, far_trace=far_trace, inline_weight=inline_weight, time_weight=time_weight, lag_low=lag_low, lag_high=lag_high, strain=strain)


BIG = 1.0e9
PENALTY = 2.0
FACE_SCALE = 0.016


def min_filter(values, radius):
    width_count = values.shape[-1]
    rim_fill = jnp.full(values.shape[:-1] + (3,), BIG, jnp.float32)
    extended = jnp.concatenate([rim_fill, values, rim_fill], axis=-1)
    result = values
    for shift_step in (1, 2, 3):
        candidate = jnp.minimum(extended[..., 3 + shift_step:3 + shift_step + width_count], extended[..., 3 - shift_step:3 - shift_step + width_count])
        result = jnp.where(shift_step <= radius, jnp.minimum(result, candidate), result)
    return result


def smooth(volume, inline_pad, time_pad):
    inline_face = FACE_SCALE * jnp.minimum(inline_pad[:-1, :], inline_pad[1:, :])[:, 1:-1]
    inline_flux = inline_face * (volume[:, 1:, 1:-1] - volume[:, :-1, 1:-1])
    time_face = FACE_SCALE * jnp.minimum(time_pad[:, :-1], time_pad[:, 1:])[1:-1, :]
    time_flux = time_face * (volume[:, 1:-1, 1:] - volume[:, 1:-1, :-1])
    centre_cells = volume[:, 1:-1, 1:-1]
    return centre_cells + inline_flux[:, 1:, :] - inline_flux[:, :-1, :] + time_flux[:, :, 1:] - time_flux[:, :, :-1]


def reference(near_trace, far_trace, inline_weight, time_weight, lag_low, lag_high, strain):
    trace_count, sample_count = near_trace.shape
    half_lags = L // 2
    padded_far = jnp.pad(far_trace, ((0, 0), (half_lags, half_lags)))
    shifted = jnp.stack([padded_far[:, lag_shift:lag_shift + sample_count] for lag_shift in range(L)])
    misfit = jnp.square(near_trace[None] - shifted)
    lag_index = lax.broadcasted_iota(jnp.int32, (L, trace_count, 1), 0)
    outside = (lag_index < lag_low[None, :, None]) | (lag_index > lag_high[None, :, None])
    misfit = misfit + PENALTY * outside.astype(jnp.float32)
    inline_pad = jnp.pad(inline_weight.astype(jnp.float32), 1)
    time_pad = jnp.pad(time_weight.astype(jnp.float32), 1)
    for sweep_index in range(ITERS):
        misfit = smooth(jnp.pad(misfit, ((0, 0), (1, 1), (1, 1))), inline_pad, time_pad)
    radius_all = jnp.repeat(strain, STRETCH, total_repeat_length=sample_count)
    sequence = jnp.transpose(misfit, (2, 1, 0))

    def advance(carried, inputs):
        sample, radius = inputs
        updated = sample + min_filter(carried, radius)
        return updated, updated

    start = jnp.zeros((trace_count, L), jnp.float32)
    unused, history = lax.scan(advance, start, (sequence, radius_all))
    history = history - jnp.min(history, axis=-1, keepdims=True)
    return jnp.transpose(history, (2, 1, 0))
```

```python
import functools

import jax
import jax.numpy as jnp
from jax import lax
from jax.experimental import pallas as pl
from jax.experimental.pallas import tpu as pltpu
from jax.sharding import PartitionSpec as P

L = 64
STRETCH = 64
ITERS = 10

BIG = 1000000000.0
PENALTY = 2.0
FACE_SCALE = 0.016

SUB = 8
LANES = 128


def neighbours(cells, axis):
    count = lax.axis_size(axis)
    ends = count - 1
    before = lax.ppermute(cells, axis, [(i, i + 1) for i in range(ends)])
    after = lax.ppermute(cells, axis, [(i + 1, i) for i in range(ends)])
    return before, after


def segments(width, reach, chunk_len):
    cuts = {0, width}
    cuts |= set(range(0, width, STRETCH))
    cuts |= {c * chunk_len - reach for c in range(1, -(-(width + reach) // chunk_len))}
    cuts = sorted(x for x in cuts if 0 <= x <= width)
    return list(zip(cuts[:-1], cuts[1:]))


def kernel(
    dims,
    far_ref,
    near_ref,
    a_ref,
    b_ref,
    bounds_ref,
    strain_ref,
    out_ref,
    m_ref,
    y_ref,
    low_ref,
    send_ref,
    recv_ref,
    send_sem,
    recv_sem,
):
    rows, width, reach, pitch, chunks, chunk_len, count = dims
    groups = L // SUB
    me = lax.axis_index("tm")
    barrier = pltpu.get_barrier_semaphore()

    @pl.when(me > 0)
    def _():
        pl.semaphore_signal(
            barrier, inc=1, device_id={"tm": me - 1}, device_id_type=pl.DeviceIdType.MESH
        )

    @pl.when(me < count - 1)
    def _():
        pl.semaphore_wait(barrier, 1)

    lane_low = bounds_ref[0:1, :]
    lane_high = bounds_ref[1:2, :]
    sub = lax.broadcasted_iota(jnp.int32, (SUB, LANES), 0)
    extra = []
    for v in range(groups):
        lag = (sub * groups + v).astype(jnp.float32)
        extra.append(jnp.where((lag < lane_low) | (lag > lane_high), PENALTY, 0.0))

    def build(j, carry):
        near = near_ref[pl.ds(j, 1), :]
        for v in range(groups):
            shifted = far_ref[pl.ds(j + v, SUB, stride=groups), :]
            diff = near - shifted
            m_ref[j, v] = diff * diff + extra[v]
        return carry

    lax.fori_loop(0, chunk_len, build, 0, unroll=2)

    last = chunk_len - 1

    def sweep(k, carry):
        first = [m_ref[0, v] for v in range(groups)]
        final = [m_ref[last, v] for v in range(groups)]
        b_last = b_ref[pl.ds(last, 1), :]
        flux = []
        for v in range(groups):
            wrapped = pltpu.roll(first[v], LANES - pitch, 1)
            m_ref[chunk_len, v] = wrapped
            flux.append(pltpu.roll(b_last * (wrapped - final[v]), pitch, 1))

        def cell(j, state):
            here, before = state
            a_row = a_ref[pl.ds(j, 1), :]
            b_row = b_ref[pl.ds(j, 1), :]
            nexts, fluxes = [], []
            for v in range(groups):
                centre = here[v]
                ahead = m_ref[j + 1, v]
                side = a_row * (pltpu.roll(centre, LANES - 1, 1) - centre)
                along = b_row * (ahead - centre)
                m_ref[j, v] = ((centre + side) - pltpu.roll(side, 1, 1)) + (along - before[v])
                nexts.append(ahead)
                fluxes.append(along)
            return nexts, fluxes

        lax.fori_loop(0, chunk_len, cell, (first, flux), unroll=2)
        return carry

    lax.fori_loop(0, ITERS, sweep, 0)

    recv_copy = pltpu.make_async_remote_copy(
        src_ref=send_ref,
        dst_ref=recv_ref,
        send_sem=send_sem,
        recv_sem=recv_sem,
        device_id={"tm": lax.min(me + 1, count - 1)},
        device_id_type=pl.DeviceIdType.MESH,
    )

    @pl.when(me == 0)
    def _():
        recv_ref[...] = jnp.zeros(recv_ref.shape, jnp.float32)

    @pl.when(me > 0)
    def _():
        recv_copy.wait_recv()

    state = [recv_ref[v] for v in range(groups)]
    lane = lax.broadcasted_iota(jnp.int32, (SUB, LANES), 1)
    at_low = sub == 0
    at_high = sub == SUB - 1
    chunk_now = 0
    for start, stop in segments(width, reach, chunk_len):
        chunk = (start + reach) // chunk_len
        if chunk != chunk_now:
            state = [pltpu.roll(x, pitch, 1) for x in state]
            chunk_now = chunk
        radius = strain_ref[start // STRETCH]
        gate2 = jnp.full((SUB, LANES), jnp.where(radius >= 2, -BIG, BIG), jnp.float32)
        gate3 = jnp.full((SUB, LANES), jnp.where(radius >= 3, -BIG, BIG), jnp.float32)
        mine = (lane >= chunk * pitch) & (lane < (chunk + 1) * pitch)

        def advance(j, x):
            wide = {v: x[v] for v in range(groups)}
            for k in range(1, 4):
                wide[-k] = jnp.where(at_low, BIG, pltpu.roll(x[groups - k], 1, 0))
                wide[groups - 1 + k] = jnp.where(at_high, BIG, pltpu.roll(x[k - 1], SUB - 1, 0))
            pair = {v: jnp.minimum(wide[v], wide[v + 1]) for v in range(-1, groups)}
            new = []
            for v in range(groups):
                near3 = jnp.minimum(pair[v - 1], pair[v])
                two = jnp.maximum(jnp.minimum(wide[v - 2], wide[v + 2]), gate2)
                three = jnp.maximum(jnp.minimum(wide[v - 3], wide[v + 3]), gate3)
                total = m_ref[j, v] + jnp.minimum(near3, jnp.minimum(two, three))
                if chunk == 0:
                    y_ref[j, v] = total
                else:
                    y_ref[j, v] = jnp.where(mine, total, y_ref[j, v])
                new.append(total)
            return new

        base = chunk * chunk_len - reach
        state = lax.fori_loop(start - base, stop - base, advance, state, unroll=2)

    @pl.when(me < count - 1)
    def _():
        for v in range(groups):
            send_ref[v] = pltpu.roll(state[v], (LANES - chunk_now * pitch) % LANES, 1)
        recv_copy.start()

    def least(j, carry):
        low = y_ref[j, 0]
        for v in range(1, groups):
            low = jnp.minimum(low, y_ref[j, v])
        low = jnp.min(low, axis=0, keepdims=True)
        low_ref[pl.ds(j, 1), :] = low
        return carry

    lax.fori_loop(0, chunk_len, least, 0, unroll=2)

    def emit(lag, carry):
        sub_index, v = lag // groups, lag % groups
        cells = y_ref[0:chunk_len, v, sub_index, :] - low_ref[0:chunk_len, :]
        flat = jnp.transpose(cells)
        parts = []
        for c in range(chunks):
            begin = max(reach - c * chunk_len, 0)
            end = min(width + reach - c * chunk_len, chunk_len)
            if end > begin:
                parts.append(flat[c * pitch + reach : c * pitch + reach + rows, begin:end])
        out_ref[lag] = jnp.concatenate(parts, axis=1)
        return carry

    for lag in range(L):
        emit(lag, 0)

    @pl.when(me < count - 1)
    def _():
        recv_copy.wait_send()


def per_device(near_trace, far_trace, inline_weight, time_weight, lag_low, lag_high, strain):
    rows, width = near_trace.shape
    half = L // 2
    reach = ITERS
    groups = L // SUB
    total_rows = rows + 2 * reach
    chunks = LANES // total_rows
    pitch = LANES // chunks
    total_cols = width + 2 * reach
    chunk_len = -(-total_cols // chunks)
    count = lax.axis_size("tm")

    fields = jnp.stack(
        [
            far_trace,
            near_trace,
            inline_weight.astype(jnp.float32),
            time_weight.astype(jnp.float32),
        ]
    )
    before, after = neighbours(fields, "tm")
    deep = half + reach
    wide = jnp.concatenate([before[:, :, width - deep :], fields, after[:, :, :deep]], axis=2)
    bounds = jnp.stack([lag_low, lag_high], axis=-1).astype(jnp.float32)
    marks = jnp.zeros((1, rows, wide.shape[2]), jnp.float32).at[0, :, :2].set(bounds)
    wide = jnp.concatenate([wide, marks], axis=0)
    count_in = lax.axis_size("inline")
    up = lax.ppermute(
        wide[:, rows - reach :], "inline", [(i, i + 1) for i in range(count_in - 1)]
    )
    down = lax.ppermute(wide[:, :reach], "inline", [(i + 1, i) for i in range(count_in - 1)])
    wide = jnp.concatenate([up, wide, down], axis=1)

    def packed(cells, length):
        need = (chunks - 1) * chunk_len + length
        cells = jnp.pad(
            cells, ((0, pitch - total_rows), (0, max(need - cells.shape[1], 0)))
        )
        lanes = jnp.concatenate(
            [cells[:, c * chunk_len : c * chunk_len + length] for c in range(chunks)], axis=0
        )
        lanes = jnp.pad(lanes, ((0, LANES - lanes.shape[0]), (0, -length % SUB)))
        return jnp.transpose(lanes)

    core = wide[:, :, half : half + total_cols]
    far_p = packed(wide[0], chunk_len + L)
    near_p = packed(core[1], chunk_len)
    inline_w, time_w = core[2], core[3]
    a_face = FACE_SCALE * jnp.minimum(inline_w, jnp.pad(inline_w[1:], ((0, 1), (0, 0))))
    b_face = FACE_SCALE * jnp.minimum(time_w, jnp.pad(time_w[:, 1:], ((0, 0), (0, 1))))
    a_p = packed(a_face, chunk_len)
    b_p = packed(b_face, chunk_len)
    line = jnp.pad(wide[4, :, :2], ((0, pitch - total_rows), (0, 0)))
    line = jnp.pad(jnp.tile(line, (chunks, 1)), ((0, LANES - chunks * pitch), (0, SUB - 2)))
    bounds_p = jnp.transpose(line)

    vmem = pl.BlockSpec(memory_space=pltpu.VMEM)
    dims = (rows, width, reach, pitch, chunks, chunk_len, count)
    padded_len = -(-chunk_len // SUB) * SUB
    return pl.pallas_call(
        functools.partial(kernel, dims),
        out_shape=jax.ShapeDtypeStruct((L, rows, width), jnp.float32),
        in_specs=[vmem] * 5 + [pl.BlockSpec(memory_space=pltpu.SMEM)],
        out_specs=vmem,
        scratch_shapes=[
            pltpu.VMEM((chunk_len + 1, groups, SUB, LANES), jnp.float32),
            pltpu.VMEM((padded_len, groups, SUB, LANES), jnp.float32),
            pltpu.VMEM((padded_len, LANES), jnp.float32),
            pltpu.VMEM((groups, SUB, LANES), jnp.float32),
            pltpu.VMEM((groups, SUB, LANES), jnp.float32),
            pltpu.SemaphoreType.DMA,
            pltpu.SemaphoreType.DMA,
        ],
        compiler_params=pltpu.CompilerParams(collective_id=0, has_side_effects=True),
    )(far_p, near_p, a_p, b_p, bounds_p, strain)


def solution(mesh):
    return jax.shard_map(
        per_device,
        mesh=mesh,
        in_specs=(
            P(("group", "inline"), "tm"),
            P(("group", "inline"), "tm"),
            P(("group", "inline"), "tm"),
            P(("group", "inline"), "tm"),
            P(("group", "inline")),
            P(("group", "inline")),
            P(("group", "tm")),
        ),
        out_specs=P(None, ("group", "inline"), "tm"),
        check_vma=False,
    )
```

```python
import functools

import jax
import jax.numpy as jnp
from jax import lax
from jax.experimental import pallas as pl
from jax.experimental.pallas import tpu as pltpu
from jax.sharding import PartitionSpec as P

L = 64
STRETCH = 64
ITERS = 10

BIG = 1000000000.0
PENALTY = 2.0
FACE_SCALE = 0.016

SUB = 8
LANES = 128


def segments(width, reach, chunk_len):
    cuts = {0, width}
    cuts |= set(range(0, width, STRETCH))
    cuts |= {c * chunk_len - reach for c in range(1, -(-(width + reach) // chunk_len))}
    cuts = sorted(x for x in cuts if 0 <= x <= width)
    return list(zip(cuts[:-1], cuts[1:]))


OFFSETS = [(di, dj) for di in (-1, 0, 1) for dj in (-1, 0, 1) if (di, dj) != (0, 0)]


def slot_of(di, dj):
    return (di + 1) * 3 + dj + 1


def kernel(
    dims,
    fields_ref,
    strain_ref,
    out_ref,
    recv_ref,
    time_ref,
    far_ref,
    near_ref,
    face_ref,
    m_ref,
    y_ref,
    low_ref,
    send_ref,
    enter_ref,
    send_sems,
    recv_sems,
    send_sem,
    recv_sem,
):
    rows, width, reach, classes, own, side_pairs, pitch, chunks, chunk_len, count, count_in = dims
    groups = L // SUB
    half = L // 2
    me = lax.axis_index("tm")
    here_in = lax.axis_index("inline")

    def present(di, dj):
        ok = None
        for step, place, total in ((di, here_in, count_in), (dj, me, count)):
            if step:
                inside = (place + step >= 0) & (place + step < total)
                ok = inside if ok is None else ok & inside
        return ok

    def device(di, dj):
        return {
            "inline": lax.clamp(0, here_in + di, count_in - 1),
            "tm": lax.clamp(0, me + dj, count - 1),
        }

    barrier = pltpu.get_barrier_semaphore()
    for di, dj in OFFSETS:

        @pl.when(present(di, dj))
        def _():
            pl.semaphore_signal(
                barrier, inc=1, device_id=device(di, dj), device_id_type=pl.DeviceIdType.MESH
            )

    beside = [
        1 + (place > 0).astype(jnp.int32) + (place < total - 1).astype(jnp.int32)
        for place, total in ((here_in, count_in), (me, count))
    ]
    pl.semaphore_wait(barrier, beside[0] * beside[1] - 1)

    def halo_copy(di, dj):
        target = slot_of(-di, -dj)
        return pltpu.make_async_remote_copy(
            src_ref=fields_ref,
            dst_ref=recv_ref.at[target],
            send_sem=send_sems.at[slot_of(di, dj)],
            recv_sem=recv_sems.at[target],
            device_id=device(di, dj),
            device_id_type=pl.DeviceIdType.MESH,
        )

    for di, dj in OFFSETS:

        @pl.when(present(di, dj))
        def _():
            halo_copy(di, dj).start()

        @pl.when(jnp.logical_not(present(di, dj)))
        def _():
            recv_ref[slot_of(di, dj)] = jnp.zeros(fields_ref.shape, jnp.float32)

    for di, dj in OFFSETS:

        @pl.when(present(di, dj))
        def _():
            halo_copy(-di, -dj).wait_recv()

    stacked = 3 * own

    def block(field, dj, parity):
        parts = []
        for di in (-1, 0, 1):
            pick = pl.ds(parity, own, stride=classes)
            if di == 0 and dj == 0:
                parts.append(fields_ref[field, pick, :])
            else:
                parts.append(recv_ref[slot_of(di, dj), field, pick, :])
        return parts

    for pair in range(2):
        for dj in (-1, 0, 1):
            parts = []
            for field in (2 * pair, 2 * pair + 1):
                for parity in range(classes):
                    parts += block(field, dj, parity)
            tall = jnp.concatenate(parts, axis=0)
            time_ref[pair, (dj + 1) * width : (dj + 2) * width, 0 : tall.shape[0]] = (
                jnp.transpose(tall)
            )

    line = lax.broadcasted_iota(jnp.int32, (1, LANES), 1)
    spot = line % pitch
    live = line < chunks * pitch
    first_time = width - reach

    def pack(pair, start, length, lane_off, step):
        size = -(-length // SUB) * SUB
        result = None
        for c in range(chunks):
            base = start + c * step
            x = time_ref[pair, base : base + size, :]
            x = pltpu.roll(x, (c * pitch - lane_off) % LANES, 1)
            result = x if c == 0 else jnp.where(line >= c * pitch, x, result)
        return jnp.where(live, result, 0.0), size

    skip = own - side_pairs
    span = own + 2 * side_pairs
    inline_rows = []
    for e in range(classes):
        far, size = pack(0, first_time - half, chunk_len + L, e * stacked + skip, chunk_len)
        far_ref[e, 0:size] = far
        near, size = pack(
            0, first_time, chunk_len, (classes + e) * stacked + skip, chunk_len
        )
        near_ref[e, 0:size] = near
        inline_rows.append(pack(1, first_time, chunk_len, e * stacked + skip, chunk_len)[0])
        time_off = (classes + e) * stacked + skip
        time_now = pack(1, first_time, chunk_len, time_off, chunk_len)[0]
        time_next = pack(1, first_time + 1, chunk_len, time_off, chunk_len)[0]
        face_ref[classes + 1 + e, 0:size] = FACE_SCALE * jnp.minimum(time_now, time_next)
    for e in range(classes):
        if e < classes - 1:
            other, inner = inline_rows[e + 1], span
        else:
            other, inner = pltpu.roll(inline_rows[0], LANES - 1, 1), span - 1
        face = jnp.where(spot < inner, FACE_SCALE * jnp.minimum(inline_rows[e], other), 0.0)
        face = jnp.where(live, face, 0.0)
        face_ref[e, 0:size] = face
        if e == classes - 1:
            face_ref[classes, 0:size] = pltpu.roll(face, 1, 1)

    sub = lax.broadcasted_iota(jnp.int32, (SUB, LANES), 0)
    extra = []
    for e in range(classes):
        marks = jnp.transpose(jnp.concatenate(block(4, 0, e) * 2, axis=0))[0:SUB]
        marks = jnp.concatenate(
            [marks, jnp.zeros((SUB, LANES - marks.shape[1]), jnp.float32)], axis=1
        )
        bounds = None
        for c in range(chunks):
            x = pltpu.roll(marks, (c * pitch - skip) % LANES, 1)
            bounds = x if c == 0 else jnp.where(line >= c * pitch, x, bounds)
        lane_low, lane_high = bounds[0:1], bounds[1:2]
        for v in range(groups):
            lag = (sub * groups + v).astype(jnp.float32)
            extra.append(jnp.where((lag < lane_low) | (lag > lane_high), PENALTY, 0.0))

    for e in range(classes):

        def build(j, carry):
            near = near_ref[e, pl.ds(j, 1), :]
            for v in range(groups):
                shifted = far_ref[e, pl.ds(j + v, SUB, stride=groups), :]
                diff = near - shifted
                m_ref[e, j, v] = diff * diff + extra[e * groups + v]
            return carry

        lax.fori_loop(0, chunk_len, build, 0, unroll=5)

    last = chunk_len - 1

    def sweep(k, carry):
        for begin in range(0, groups, 4):
            picks = [(e, v) for e in range(classes) for v in range(begin, begin + 4)]
            first = {p: m_ref[p[0], 0, p[1]] for p in picks}
            flux = {}
            for p in picks:
                e, v = p
                wrapped = pltpu.roll(first[p], LANES - pitch, 1)
                m_ref[e, chunk_len, v] = wrapped
                b_last = face_ref[classes + 1 + e, pl.ds(last, 1), :]
                flux[p] = pltpu.roll(b_last * (wrapped - m_ref[e, last, v]), pitch, 1)

            def cell(j, state):
                here, before = state
                here = dict(zip(picks, here))
                before = dict(zip(picks, before))
                a_rows = [face_ref[e, pl.ds(j, 1), :] for e in range(classes + 1)]
                b_rows = [face_ref[classes + 1 + e, pl.ds(j, 1), :] for e in range(classes)]
                nexts, fluxes = [], []
                links = {}
                for e, v in picks:
                    if e < classes - 1:
                        links[e, v] = a_rows[e] * (here[e + 1, v] - here[e, v])
                    else:
                        up = pltpu.roll(here[0, v], LANES - 1, 1)
                        links[e, v] = a_rows[e] * (up - here[e, v])
                        down = pltpu.roll(here[e, v], 1, 1)
                        links[-1, v] = a_rows[classes] * (here[0, v] - down)
                for p in picks:
                    e, v = p
                    ahead = m_ref[e, j + 1, v]
                    along = b_rows[e] * (ahead - here[p])
                    m_ref[e, j, v] = ((here[p] + links[e, v]) - links[e - 1, v]) + (
                        along - before[p]
                    )
                    nexts.append(ahead)
                    fluxes.append(along)
                return nexts, fluxes

            lax.fori_loop(
                0,
                chunk_len,
                cell,
                ([first[p] for p in picks], [flux[p] for p in picks]),
                unroll=5,
            )
        return carry

    lax.fori_loop(0, ITERS, sweep, 0)

    owned = (spot >= side_pairs) & (spot < side_pairs + own) & live

    def merge(j, carry):
        for v in range(groups):
            other = pltpu.roll(m_ref[1, j, v], own, 1)
            m_ref[0, j, v] = jnp.where(owned, m_ref[0, j, v], other)
        return carry

    if classes == 2:
        lax.fori_loop(0, chunk_len, merge, 0, unroll=5)

    state_copy = pltpu.make_async_remote_copy(
        src_ref=send_ref,
        dst_ref=enter_ref,
        send_sem=send_sem,
        recv_sem=recv_sem,
        device_id={"tm": lax.min(me + 1, count - 1)},
        device_id_type=pl.DeviceIdType.MESH,
    )

    @pl.when(me == 0)
    def _():
        enter_ref[...] = jnp.zeros(enter_ref.shape, jnp.float32)

    @pl.when(me > 0)
    def _():
        state_copy.wait_recv()

    state = [enter_ref[v] for v in range(groups)]
    lane = lax.broadcasted_iota(jnp.int32, (SUB, LANES), 1)
    at_low = sub == 0
    at_high = sub == SUB - 1
    chunk_now = 0
    for start, stop in segments(width, reach, chunk_len):
        chunk = (start + reach) // chunk_len
        if chunk != chunk_now:
            state = [pltpu.roll(x, pitch, 1) for x in state]
            chunk_now = chunk
        radius = strain_ref[start // STRETCH]
        gate2 = jnp.full((SUB, LANES), jnp.where(radius >= 2, -BIG, BIG), jnp.float32)
        gate3 = jnp.full((SUB, LANES), jnp.where(radius >= 3, -BIG, BIG), jnp.float32)
        mine = lax.rem(lane + (LANES - side_pairs) + LANES - chunk * pitch, LANES) < rows

        def advance(j, x):
            wide = {v: x[v] for v in range(groups)}
            for k in range(1, 4):
                wide[-k] = jnp.where(at_low, BIG, pltpu.roll(x[groups - k], 1, 0))
                wide[groups - 1 + k] = jnp.where(at_high, BIG, pltpu.roll(x[k - 1], SUB - 1, 0))
            pair = {v: jnp.minimum(wide[v], wide[v + 1]) for v in range(-1, groups)}
            new = []
            for v in range(groups):
                near3 = jnp.minimum(pair[v - 1], pair[v])
                two = jnp.maximum(jnp.minimum(wide[v - 2], wide[v + 2]), gate2)
                three = jnp.maximum(jnp.minimum(wide[v - 3], wide[v + 3]), gate3)
                total = m_ref[0, j, v] + jnp.minimum(near3, jnp.minimum(two, three))
                if chunk == 0:
                    y_ref[j, v] = total
                else:
                    y_ref[j, v] = jnp.where(mine, total, y_ref[j, v])
                new.append(total)
            return new

        base = chunk * chunk_len - reach
        state = lax.fori_loop(start - base, stop - base, advance, state, unroll=4)

    @pl.when(me < count - 1)
    def _():
        for v in range(groups):
            send_ref[v] = pltpu.roll(state[v], (LANES - chunk_now * pitch) % LANES, 1)
        state_copy.start()

    def least(j, carry):
        low = y_ref[j, 0]
        for v in range(1, groups):
            low = jnp.minimum(low, y_ref[j, v])
        low = jnp.min(low, axis=0, keepdims=True)
        low_ref[pl.ds(j, 1), :] = low
        return carry

    lax.fori_loop(0, chunk_len, least, 0, unroll=5)

    for lag in range(L):
        sub_index, v = lag // groups, lag % groups
        cells = y_ref[0:chunk_len, v, sub_index, :] - low_ref[0:chunk_len, :]
        flat = jnp.transpose(cells)
        flat = jnp.concatenate([flat, flat[0 : 2 * SUB]], axis=0)
        for e in range(classes):
            parts = []
            for c in range(chunks):
                begin = max(reach - c * chunk_len, 0)
                end = min(width + reach - c * chunk_len, chunk_len)
                if end > begin:
                    at = c * pitch + side_pairs + e * own
                    parts.append(flat[at : at + own, begin:end])
            out_ref[lag, pl.ds(e, own, stride=classes), :] = jnp.concatenate(parts, axis=1)

    @pl.when(me < count - 1)
    def _():
        state_copy.wait_send()

    for di, dj in OFFSETS:

        @pl.when(present(di, dj))
        def _():
            halo_copy(di, dj).wait_send()


def per_device(near_trace, far_trace, inline_weight, time_weight, lag_low, lag_high, strain):
    rows, width = near_trace.shape
    reach = ITERS
    groups = L // SUB
    classes = 2
    own = rows // classes
    side_pairs = -(-reach // classes)
    pitch = -(-(rows + side_pairs) // 1)
    chunks = LANES // pitch
    chunk_len = -(-(width + 2 * reach) // chunks)
    count = lax.axis_size("tm")
    count_in = lax.axis_size("inline")

    mark = lax.broadcasted_iota(jnp.int32, (rows, width), 1)
    bounds = jnp.where(mark == 0, lag_low[:, None], lag_high[:, None])
    fields = jnp.stack(
        [
            far_trace,
            near_trace,
            inline_weight.astype(jnp.float32),
            time_weight.astype(jnp.float32),
            bounds.astype(jnp.float32),
        ]
    )
    vmem = pl.BlockSpec(memory_space=pltpu.VMEM)
    dims = (
        rows,
        width,
        reach,
        classes,
        own,
        side_pairs,
        pitch,
        chunks,
        chunk_len,
        count,
        count_in,
    )
    whole = -(-chunk_len // SUB) * SUB
    deep = -(-(chunk_len + L) // SUB) * SUB
    return pl.pallas_call(
        functools.partial(kernel, dims),
        out_shape=jax.ShapeDtypeStruct((L, rows, width), jnp.float32),
        in_specs=[vmem, pl.BlockSpec(memory_space=pltpu.SMEM)],
        out_specs=vmem,
        scratch_shapes=[
            pltpu.VMEM((9,) + fields.shape, jnp.float32),
            pltpu.VMEM((2, 3 * width, LANES), jnp.float32),
            pltpu.VMEM((classes, deep, LANES), jnp.float32),
            pltpu.VMEM((classes, whole, LANES), jnp.float32),
            pltpu.VMEM((2 * classes + 1, whole, LANES), jnp.float32),
            pltpu.VMEM((classes, chunk_len + 1, groups, SUB, LANES), jnp.float32),
            pltpu.VMEM((whole, groups, SUB, LANES), jnp.float32),
            pltpu.VMEM((whole, LANES), jnp.float32),
            pltpu.VMEM((groups, SUB, LANES), jnp.float32),
            pltpu.VMEM((groups, SUB, LANES), jnp.float32),
            pltpu.SemaphoreType.DMA((9,)),
            pltpu.SemaphoreType.DMA((9,)),
            pltpu.SemaphoreType.DMA,
            pltpu.SemaphoreType.DMA,
        ],
        compiler_params=pltpu.CompilerParams(collective_id=0, has_side_effects=True),
    )(fields, strain)


def solution(mesh):
    return jax.shard_map(
        per_device,
        mesh=mesh,
        in_specs=(
            P(("group", "inline"), "tm"),
            P(("group", "inline"), "tm"),
            P(("group", "inline"), "tm"),
            P(("group", "inline"), "tm"),
            P(("group", "inline")),
            P(("group", "inline")),
            P(("group", "tm")),
        ),
        out_specs=P(None, ("group", "inline"), "tm"),
        check_vma=False,
    )
```

```python
import functools

import jax
import jax.numpy as jnp
from jax import lax
from jax.experimental import pallas as pl
from jax.experimental.pallas import tpu as pltpu
from jax.sharding import PartitionSpec as P

L = 64
STRETCH = 64
ITERS = 10

BIG = 1000000000.0
PENALTY = 2.0
FACE_SCALE = 0.016

SUB = 8
LANES = 128


def segments(width, reach, chunk_len):
    cuts = {0, width}
    cuts |= set(range(0, width, STRETCH))
    cuts |= {c * chunk_len - reach for c in range(1, -(-(width + reach) // chunk_len))}
    cuts = sorted(x for x in cuts if 0 <= x <= width)
    return list(zip(cuts[:-1], cuts[1:]))


OFFSETS = [(di, dj) for di in (-1, 0, 1) for dj in (-1, 0, 1) if (di, dj) != (0, 0)]


def slot_of(di, dj):
    return (di + 1) * 3 + dj + 1


def kernel(
    dims,
    fields_ref,
    strain_ref,
    out_ref,
    recv_ref,
    time_ref,
    far_ref,
    near_ref,
    face_ref,
    m_ref,
    y_ref,
    low_ref,
    send_ref,
    enter_ref,
    send_sems,
    recv_sems,
    send_sem,
    recv_sem,
):
    rows, width, reach, classes, own, side_pairs, pitch, chunks, chunk_len, count, count_in = dims
    groups = L // SUB
    half = L // 2
    me = lax.axis_index("tm")
    here_in = lax.axis_index("inline")

    def present(di, dj):
        ok = None
        for step, place, total in ((di, here_in, count_in), (dj, me, count)):
            if step:
                inside = (place + step >= 0) & (place + step < total)
                ok = inside if ok is None else ok & inside
        return ok

    def device(di, dj):
        return {
            "inline": lax.clamp(0, here_in + di, count_in - 1),
            "tm": lax.clamp(0, me + dj, count - 1),
        }

    barrier = pltpu.get_barrier_semaphore()
    for di, dj in OFFSETS:

        @pl.when(present(di, dj))
        def _():
            pl.semaphore_signal(
                barrier, inc=1, device_id=device(di, dj), device_id_type=pl.DeviceIdType.MESH
            )

    beside = [
        1 + (place > 0).astype(jnp.int32) + (place < total - 1).astype(jnp.int32)
        for place, total in ((here_in, count_in), (me, count))
    ]
    pl.semaphore_wait(barrier, beside[0] * beside[1] - 1)

    def halo_copy(di, dj):
        target = slot_of(-di, -dj)
        return pltpu.make_async_remote_copy(
            src_ref=fields_ref,
            dst_ref=recv_ref.at[target],
            send_sem=send_sems.at[slot_of(di, dj)],
            recv_sem=recv_sems.at[target],
            device_id=device(di, dj),
            device_id_type=pl.DeviceIdType.MESH,
        )

    for di, dj in OFFSETS:

        @pl.when(present(di, dj))
        def _():
            halo_copy(di, dj).start()

        @pl.when(jnp.logical_not(present(di, dj)))
        def _():
            recv_ref[slot_of(di, dj)] = jnp.zeros(fields_ref.shape, jnp.float32)

    for di, dj in OFFSETS:

        @pl.when(present(di, dj))
        def _():
            halo_copy(-di, -dj).wait_recv()

    stacked = 3 * own

    def block(field, dj, parity):
        parts = []
        for di in (-1, 0, 1):
            pick = pl.ds(parity, own, stride=classes)
            if di == 0 and dj == 0:
                parts.append(fields_ref[field, pick, :])
            else:
                parts.append(recv_ref[slot_of(di, dj), field, pick, :])
        return parts

    for pair in range(2):
        for dj in (-1, 0, 1):
            parts = []
            for field in (2 * pair, 2 * pair + 1):
                for parity in range(classes):
                    parts += block(field, dj, parity)
            tall = jnp.concatenate(parts, axis=0)
            time_ref[pair, (dj + 1) * width : (dj + 2) * width, 0 : tall.shape[0]] = (
                jnp.transpose(tall)
            )

    line = lax.broadcasted_iota(jnp.int32, (1, LANES), 1)
    spot = line % pitch
    live = line < chunks * pitch
    first_time = width - reach

    def pack(pair, start, length, lane_off, step):
        size = -(-length // SUB) * SUB
        result = None
        for c in range(chunks):
            base = start + c * step
            x = time_ref[pair, base : base + size, :]
            x = pltpu.roll(x, (c * pitch - lane_off) % LANES, 1)
            result = x if c == 0 else jnp.where(line >= c * pitch, x, result)
        return jnp.where(live, result, 0.0), size

    skip = own - side_pairs
    span = own + 2 * side_pairs
    inline_rows = []
    for e in range(classes):
        far, size = pack(0, first_time - half, chunk_len + L, e * stacked + skip, chunk_len)
        far_ref[e, 0:size] = far
        near, size = pack(
            0, first_time, chunk_len, (classes + e) * stacked + skip, chunk_len
        )
        near_ref[e, 0:size] = near
        inline_rows.append(pack(1, first_time, chunk_len, e * stacked + skip, chunk_len)[0])
        time_off = (classes + e) * stacked + skip
        time_now = pack(1, first_time, chunk_len, time_off, chunk_len)[0]
        time_next = pack(1, first_time + 1, chunk_len, time_off, chunk_len)[0]
        face_ref[classes + 1 + e, 0:size] = FACE_SCALE * jnp.minimum(time_now, time_next)
    for e in range(classes):
        if e < classes - 1:
            other, inner = inline_rows[e + 1], span
        else:
            other, inner = pltpu.roll(inline_rows[0], LANES - 1, 1), span - 1
        face = jnp.where(spot < inner, FACE_SCALE * jnp.minimum(inline_rows[e], other), 0.0)
        face = jnp.where(live, face, 0.0)
        face_ref[e, 0:size] = face
        if e == classes - 1:
            face_ref[classes, 0:size] = pltpu.roll(face, 1, 1)

    sub = lax.broadcasted_iota(jnp.int32, (SUB, LANES), 0)
    extra = []
    for e in range(classes):
        marks = jnp.transpose(jnp.concatenate(block(4, 0, e) * 2, axis=0))[0:SUB]
        marks = jnp.concatenate(
            [marks, jnp.zeros((SUB, LANES - marks.shape[1]), jnp.float32)], axis=1
        )
        bounds = None
        for c in range(chunks):
            x = pltpu.roll(marks, (c * pitch - skip) % LANES, 1)
            bounds = x if c == 0 else jnp.where(line >= c * pitch, x, bounds)
        lane_low, lane_high = bounds[0:1], bounds[1:2]
        for v in range(groups):
            lag = (sub * groups + v).astype(jnp.float32)
            extra.append(jnp.where((lag < lane_low) | (lag > lane_high), PENALTY, 0.0))

    for e in range(classes):

        def build(j, carry):
            near = near_ref[e, pl.ds(j, 1), :]
            for v in range(groups):
                shifted = far_ref[e, pl.ds(j + v, SUB, stride=groups), :]
                diff = near - shifted
                m_ref[e, j, v] = diff * diff + extra[e * groups + v]
            return carry

        lax.fori_loop(0, chunk_len, build, 0, unroll=5)

    last = chunk_len - 1

    def sweep(k, carry):
        for begin in range(0, groups, 4):
            picks = [(e, v) for e in range(classes) for v in range(begin, begin + 4)]
            first = {p: m_ref[p[0], 0, p[1]] for p in picks}
            flux = {}
            for p in picks:
                e, v = p
                wrapped = pltpu.roll(first[p], LANES - pitch, 1)
                m_ref[e, chunk_len, v] = wrapped
                b_last = face_ref[classes + 1 + e, pl.ds(last, 1), :]
                flux[p] = pltpu.roll(b_last * (wrapped - m_ref[e, last, v]), pitch, 1)

            def cell(j, state):
                here, before = state
                here = dict(zip(picks, here))
                before = dict(zip(picks, before))
                a_rows = [face_ref[e, pl.ds(j, 1), :] for e in range(classes + 1)]
                b_rows = [face_ref[classes + 1 + e, pl.ds(j, 1), :] for e in range(classes)]
                nexts, fluxes = [], []
                links = {}
                for e, v in picks:
                    if e < classes - 1:
                        links[e, v] = a_rows[e] * (here[e + 1, v] - here[e, v])
                    else:
                        up = pltpu.roll(here[0, v], LANES - 1, 1)
                        links[e, v] = a_rows[e] * (up - here[e, v])
                        down = pltpu.roll(here[e, v], 1, 1)
                        links[-1, v] = a_rows[classes] * (here[0, v] - down)
                for p in picks:
                    e, v = p
                    ahead = m_ref[e, j + 1, v]
                    along = b_rows[e] * (ahead - here[p])
                    m_ref[e, j, v] = ((here[p] + links[e, v]) - links[e - 1, v]) + (
                        along - before[p]
                    )
                    nexts.append(ahead)
                    fluxes.append(along)
                return nexts, fluxes

            lax.fori_loop(
                0,
                chunk_len,
                cell,
                ([first[p] for p in picks], [flux[p] for p in picks]),
                unroll=chunk_len,
            )
        return carry

    lax.fori_loop(0, ITERS, sweep, 0)

    owned = (spot >= side_pairs) & (spot < side_pairs + own) & live

    def merge(j, carry):
        for v in range(groups):
            other = pltpu.roll(m_ref[1, j, v], own, 1)
            m_ref[0, j, v] = jnp.where(owned, m_ref[0, j, v], other)
        return carry

    if classes == 2:
        lax.fori_loop(0, chunk_len, merge, 0, unroll=5)

    state_copy = pltpu.make_async_remote_copy(
        src_ref=send_ref,
        dst_ref=enter_ref,
        send_sem=send_sem,
        recv_sem=recv_sem,
        device_id={"tm": lax.min(me + 1, count - 1)},
        device_id_type=pl.DeviceIdType.MESH,
    )

    @pl.when(me == 0)
    def _():
        enter_ref[...] = jnp.zeros(enter_ref.shape, jnp.float32)

    @pl.when(me > 0)
    def _():
        state_copy.wait_recv()

    state = [enter_ref[v] for v in range(groups)]
    lane = lax.broadcasted_iota(jnp.int32, (SUB, LANES), 1)
    at_low = sub == 0
    at_high = sub == SUB - 1
    chunk_now = 0
    for start, stop in segments(width, reach, chunk_len):
        chunk = (start + reach) // chunk_len
        if chunk != chunk_now:
            state = [pltpu.roll(x, pitch, 1) for x in state]
            chunk_now = chunk
        radius = strain_ref[start // STRETCH]
        gate2 = jnp.full((SUB, LANES), jnp.where(radius >= 2, -BIG, BIG), jnp.float32)
        gate3 = jnp.full((SUB, LANES), jnp.where(radius >= 3, -BIG, BIG), jnp.float32)
        mine = lax.rem(lane + (LANES - side_pairs) + LANES - chunk * pitch, LANES) < rows

        def advance(j, x):
            wide = {v: x[v] for v in range(groups)}
            for k in range(1, 4):
                wide[-k] = jnp.where(at_low, BIG, pltpu.roll(x[groups - k], 1, 0))
                wide[groups - 1 + k] = jnp.where(at_high, BIG, pltpu.roll(x[k - 1], SUB - 1, 0))
            pair = {v: jnp.minimum(wide[v], wide[v + 1]) for v in range(-1, groups)}
            new = []
            for v in range(groups):
                near3 = jnp.minimum(pair[v - 1], pair[v])
                two = jnp.maximum(jnp.minimum(wide[v - 2], wide[v + 2]), gate2)
                three = jnp.maximum(jnp.minimum(wide[v - 3], wide[v + 3]), gate3)
                total = m_ref[0, j, v] + jnp.minimum(near3, jnp.minimum(two, three))
                if chunk == 0:
                    y_ref[j, v] = total
                else:
                    y_ref[j, v] = jnp.where(mine, total, y_ref[j, v])
                new.append(total)
            return new

        base = chunk * chunk_len - reach
        state = lax.fori_loop(start - base, stop - base, advance, state, unroll=stop - start)

    @pl.when(me < count - 1)
    def _():
        for v in range(groups):
            send_ref[v] = pltpu.roll(state[v], (LANES - chunk_now * pitch) % LANES, 1)
        state_copy.start()

    def least(j, carry):
        low = y_ref[j, 0]
        for v in range(1, groups):
            low = jnp.minimum(low, y_ref[j, v])
        low = jnp.min(low, axis=0, keepdims=True)
        low_ref[pl.ds(j, 1), :] = low
        return carry

    lax.fori_loop(0, chunk_len, least, 0, unroll=5)

    for lag in range(L):
        sub_index, v = lag // groups, lag % groups
        cells = y_ref[0:chunk_len, v, sub_index, :] - low_ref[0:chunk_len, :]
        flat = jnp.transpose(cells)
        flat = jnp.concatenate([flat, flat[0 : 2 * SUB]], axis=0)
        for e in range(classes):
            parts = []
            for c in range(chunks):
                begin = max(reach - c * chunk_len, 0)
                end = min(width + reach - c * chunk_len, chunk_len)
                if end > begin:
                    at = c * pitch + side_pairs + e * own
                    parts.append(flat[at : at + own, begin:end])
            out_ref[lag, pl.ds(e, own, stride=classes), :] = jnp.concatenate(parts, axis=1)

    @pl.when(me < count - 1)
    def _():
        state_copy.wait_send()

    for di, dj in OFFSETS:

        @pl.when(present(di, dj))
        def _():
            halo_copy(di, dj).wait_send()


def per_device(near_trace, far_trace, inline_weight, time_weight, lag_low, lag_high, strain):
    rows, width = near_trace.shape
    reach = ITERS
    groups = L // SUB
    classes = 2
    own = rows // classes
    side_pairs = -(-reach // classes)
    pitch = -(-(rows + side_pairs) // 1)
    chunks = LANES // pitch
    chunk_len = -(-(width + 2 * reach) // chunks)
    count = lax.axis_size("tm")
    count_in = lax.axis_size("inline")

    mark = lax.broadcasted_iota(jnp.int32, (rows, width), 1)
    bounds = jnp.where(mark == 0, lag_low[:, None], lag_high[:, None])
    fields = jnp.stack(
        [
            far_trace,
            near_trace,
            inline_weight.astype(jnp.float32),
            time_weight.astype(jnp.float32),
            bounds.astype(jnp.float32),
        ]
    )
    vmem = pl.BlockSpec(memory_space=pltpu.VMEM)
    dims = (
        rows,
        width,
        reach,
        classes,
        own,
        side_pairs,
        pitch,
        chunks,
        chunk_len,
        count,
        count_in,
    )
    whole = -(-chunk_len // SUB) * SUB
    deep = -(-(chunk_len + L) // SUB) * SUB
    return pl.pallas_call(
        functools.partial(kernel, dims),
        out_shape=jax.ShapeDtypeStruct((L, rows, width), jnp.float32),
        in_specs=[vmem, pl.BlockSpec(memory_space=pltpu.SMEM)],
        out_specs=vmem,
        scratch_shapes=[
            pltpu.VMEM((9,) + fields.shape, jnp.float32),
            pltpu.VMEM((2, 3 * width, LANES), jnp.float32),
            pltpu.VMEM((classes, deep, LANES), jnp.float32),
            pltpu.VMEM((classes, whole, LANES), jnp.float32),
            pltpu.VMEM((2 * classes + 1, whole, LANES), jnp.float32),
            pltpu.VMEM((classes, chunk_len + 1, groups, SUB, LANES), jnp.float32),
            pltpu.VMEM((whole, groups, SUB, LANES), jnp.float32),
            pltpu.VMEM((whole, LANES), jnp.float32),
            pltpu.VMEM((groups, SUB, LANES), jnp.float32),
            pltpu.VMEM((groups, SUB, LANES), jnp.float32),
            pltpu.SemaphoreType.DMA((9,)),
            pltpu.SemaphoreType.DMA((9,)),
            pltpu.SemaphoreType.DMA,
            pltpu.SemaphoreType.DMA,
        ],
        compiler_params=pltpu.CompilerParams(collective_id=0, has_side_effects=True),
    )(fields, strain)


def solution(mesh):
    return jax.shard_map(
        per_device,
        mesh=mesh,
        in_specs=(
            P(("group", "inline"), "tm"),
            P(("group", "inline"), "tm"),
            P(("group", "inline"), "tm"),
            P(("group", "inline"), "tm"),
            P(("group", "inline")),
            P(("group", "inline")),
            P(("group", "tm")),
        ),
        out_specs=P(None, ("group", "inline"), "tm"),
        check_vma=False,
    )
```

```python
import functools

import jax
import jax.numpy as jnp
from jax import lax
from jax.experimental import pallas as pl
from jax.experimental.pallas import tpu as pltpu
from jax.sharding import PartitionSpec as P

L = 64
STRETCH = 64
ITERS = 10

BIG = 1000000000.0
PENALTY = 2.0
FACE_SCALE = 0.016

SUB = 8
LANES = 128


def segments(width, reach, chunk_len):
    cuts = {0, width}
    cuts |= set(range(0, width, STRETCH))
    cuts |= {c * chunk_len - reach for c in range(1, -(-(width + reach) // chunk_len))}
    cuts = sorted(x for x in cuts if 0 <= x <= width)
    return list(zip(cuts[:-1], cuts[1:]))


OFFSETS = [(di, dj) for di in (-1, 0, 1) for dj in (-1, 0, 1) if (di, dj) != (0, 0)]


def slot_of(di, dj):
    return (di + 1) * 3 + dj + 1


def kernel(
    dims,
    far_in,
    near_in,
    inline_in,
    time_in,
    bounds_in,
    strain_ref,
    out_ref,
    trace_ref,
    weight_ref,
    trace_recv,
    weight_recv,
    time_ref,
    far_ref,
    near_ref,
    face_ref,
    m_ref,
    y_ref,
    low_ref,
    send_ref,
    enter_ref,
    local_sems,
    send_sems,
    recv_sems,
    send_sem,
    recv_sem,
):
    rows, width, reach, classes, own, side_pairs, pitch, chunks, chunk_len, count, count_in = dims
    groups = L // SUB
    half = L // 2
    me = lax.axis_index("tm")
    here_in = lax.axis_index("inline")

    def present(di, dj):
        ok = None
        for step, place, total in ((di, here_in, count_in), (dj, me, count)):
            if step:
                inside = (place + step >= 0) & (place + step < total)
                ok = inside if ok is None else ok & inside
        return ok

    def device(di, dj):
        return {
            "inline": lax.clamp(0, here_in + di, count_in - 1),
            "tm": lax.clamp(0, me + dj, count - 1),
        }

    local = [
        pltpu.make_async_copy(source, target, local_sems.at[k])
        for k, (source, target) in enumerate(
            (
                (far_in, trace_ref.at[0]),
                (near_in, trace_ref.at[1]),
                (inline_in, weight_ref.at[0]),
                (time_in, weight_ref.at[1]),
                (bounds_in, weight_ref.at[2]),
            )
        )
    ]
    for copy in local:
        copy.start()

    barrier = pltpu.get_barrier_semaphore()
    for di, dj in OFFSETS:

        @pl.when(present(di, dj))
        def _():
            pl.semaphore_signal(
                barrier, inc=1, device_id=device(di, dj), device_id_type=pl.DeviceIdType.MESH
            )

    beside = [
        1 + (place > 0).astype(jnp.int32) + (place < total - 1).astype(jnp.int32)
        for place, total in ((here_in, count_in), (me, count))
    ]
    pl.semaphore_wait(barrier, beside[0] * beside[1] - 1)

    def halo_copies(di, dj):
        target = slot_of(-di, -dj)
        return [
            pltpu.make_async_remote_copy(
                src_ref=source,
                dst_ref=landing.at[target],
                send_sem=send_sems.at[kind, slot_of(di, dj)],
                recv_sem=recv_sems.at[kind, target],
                device_id=device(di, dj),
                device_id_type=pl.DeviceIdType.MESH,
            )
            for kind, (source, landing) in enumerate(
                ((trace_ref, trace_recv), (weight_ref, weight_recv))
            )
        ]

    for copy in local:
        copy.wait()

    for di, dj in OFFSETS:

        @pl.when(present(di, dj))
        def _():
            for copy in halo_copies(di, dj):
                copy.start()

        @pl.when(jnp.logical_not(present(di, dj)))
        def _():
            trace_recv[slot_of(di, dj)] = jnp.zeros(trace_ref.shape, jnp.float32)
            weight_recv[slot_of(di, dj)] = jnp.zeros(weight_ref.shape, jnp.int32)

    for di, dj in OFFSETS:

        @pl.when(present(di, dj))
        def _():
            for copy in halo_copies(-di, -dj):
                copy.wait_recv()

    stacked = 3 * own

    def block(field, dj, parity):
        parts = []
        for di in (-1, 0, 1):
            pick = pl.ds(parity, own, stride=classes)
            own_ref, landing = (trace_ref, trace_recv) if field < 2 else (weight_ref, weight_recv)
            if di == 0 and dj == 0:
                cells = own_ref[field % 2 if field < 4 else 2, pick, :]
            else:
                cells = landing[slot_of(di, dj), field % 2 if field < 4 else 2, pick, :]
            parts.append(cells.astype(jnp.float32))
        return parts

    for pair in range(2):
        for dj in (-1, 0, 1):
            parts = []
            for field in (2 * pair, 2 * pair + 1):
                for parity in range(classes):
                    parts += block(field, dj, parity)
            tall = jnp.concatenate(parts, axis=0)
            time_ref[pair, (dj + 1) * width : (dj + 2) * width, 0 : tall.shape[0]] = (
                jnp.transpose(tall)
            )

    line = lax.broadcasted_iota(jnp.int32, (1, LANES), 1)
    spot = line % pitch
    live = line < chunks * pitch
    first_time = width - reach

    def pack(pair, start, length, lane_off, step):
        size = -(-length // SUB) * SUB
        result = None
        for c in range(chunks):
            base = start + c * step
            x = time_ref[pair, base : base + size, :]
            x = pltpu.roll(x, (c * pitch - lane_off) % LANES, 1)
            result = x if c == 0 else jnp.where(line >= c * pitch, x, result)
        return jnp.where(live, result, 0.0), size

    skip = own - side_pairs
    span = own + 2 * side_pairs
    inline_rows = []
    for e in range(classes):
        far, size = pack(0, first_time - half, chunk_len + L, e * stacked + skip, chunk_len)
        far_ref[e, 0:size] = far
        near, size = pack(
            0, first_time, chunk_len, (classes + e) * stacked + skip, chunk_len
        )
        near_ref[e, 0:size] = near
        inline_rows.append(pack(1, first_time, chunk_len, e * stacked + skip, chunk_len)[0])
        time_off = (classes + e) * stacked + skip
        time_now = pack(1, first_time, chunk_len, time_off, chunk_len)[0]
        time_next = pack(1, first_time + 1, chunk_len, time_off, chunk_len)[0]
        face_ref[classes + 1 + e, 0:size] = FACE_SCALE * jnp.minimum(time_now, time_next)
    for e in range(classes):
        if e < classes - 1:
            other, inner = inline_rows[e + 1], span
        else:
            other, inner = pltpu.roll(inline_rows[0], LANES - 1, 1), span - 1
        face = jnp.where(spot < inner, FACE_SCALE * jnp.minimum(inline_rows[e], other), 0.0)
        face = jnp.where(live, face, 0.0)
        face_ref[e, 0:size] = face
        if e == classes - 1:
            face_ref[classes, 0:size] = pltpu.roll(face, 1, 1)

    sub = lax.broadcasted_iota(jnp.int32, (SUB, LANES), 0)
    extra = []
    for e in range(classes):
        marks = jnp.transpose(jnp.concatenate(block(4, 0, e) * 2, axis=0))[0:SUB]
        marks = jnp.concatenate(
            [marks, jnp.zeros((SUB, LANES - marks.shape[1]), jnp.float32)], axis=1
        )
        bounds = None
        for c in range(chunks):
            x = pltpu.roll(marks, (c * pitch - skip) % LANES, 1)
            bounds = x if c == 0 else jnp.where(line >= c * pitch, x, bounds)
        lane_low, lane_high = bounds[0:1], bounds[1:2]
        for v in range(groups):
            lag = (sub * groups + v).astype(jnp.float32)
            extra.append(jnp.where((lag < lane_low) | (lag > lane_high), PENALTY, 0.0))

    for e in range(classes):

        def build(j, carry):
            near = near_ref[e, pl.ds(j, 1), :]
            for v in range(groups):
                shifted = far_ref[e, pl.ds(j + v, SUB, stride=groups), :]
                diff = near - shifted
                m_ref[e, j, v] = diff * diff + extra[e * groups + v]
            return carry

        lax.fori_loop(0, chunk_len, build, 0, unroll=5)

    last = chunk_len - 1

    def sweep(k, carry):
        for begin in range(0, groups, 4):
            picks = [(e, v) for e in range(classes) for v in range(begin, begin + 4)]
            first = {p: m_ref[p[0], 0, p[1]] for p in picks}
            flux = {}
            for p in picks:
                e, v = p
                wrapped = pltpu.roll(first[p], LANES - pitch, 1)
                m_ref[e, chunk_len, v] = wrapped
                b_last = face_ref[classes + 1 + e, pl.ds(last, 1), :]
                flux[p] = pltpu.roll(b_last * (wrapped - m_ref[e, last, v]), pitch, 1)

            def cell(j, state):
                here, before = state
                here = dict(zip(picks, here))
                before = dict(zip(picks, before))
                a_rows = [face_ref[e, pl.ds(j, 1), :] for e in range(classes + 1)]
                b_rows = [face_ref[classes + 1 + e, pl.ds(j, 1), :] for e in range(classes)]
                nexts, fluxes = [], []
                links = {}
                for e, v in picks:
                    if e < classes - 1:
                        links[e, v] = a_rows[e] * (here[e + 1, v] - here[e, v])
                    else:
                        up = pltpu.roll(here[0, v], LANES - 1, 1)
                        links[e, v] = a_rows[e] * (up - here[e, v])
                        down = pltpu.roll(here[e, v], 1, 1)
                        links[-1, v] = a_rows[classes] * (here[0, v] - down)
                for p in picks:
                    e, v = p
                    ahead = m_ref[e, j + 1, v]
                    along = b_rows[e] * (ahead - here[p])
                    m_ref[e, j, v] = ((here[p] + links[e, v]) - links[e - 1, v]) + (
                        along - before[p]
                    )
                    nexts.append(ahead)
                    fluxes.append(along)
                return nexts, fluxes

            lax.fori_loop(
                0,
                chunk_len,
                cell,
                ([first[p] for p in picks], [flux[p] for p in picks]),
                unroll=chunk_len,
            )
        return carry

    lax.fori_loop(0, ITERS, sweep, 0)

    owned = (spot >= side_pairs) & (spot < side_pairs + own) & live

    def merge(j, carry):
        for v in range(groups):
            other = pltpu.roll(m_ref[1, j, v], own, 1)
            m_ref[0, j, v] = jnp.where(owned, m_ref[0, j, v], other)
        return carry

    if classes == 2:
        lax.fori_loop(0, chunk_len, merge, 0, unroll=5)

    state_copy = pltpu.make_async_remote_copy(
        src_ref=send_ref,
        dst_ref=enter_ref,
        send_sem=send_sem,
        recv_sem=recv_sem,
        device_id={"tm": lax.min(me + 1, count - 1)},
        device_id_type=pl.DeviceIdType.MESH,
    )

    @pl.when(me == 0)
    def _():
        enter_ref[...] = jnp.zeros(enter_ref.shape, jnp.float32)

    @pl.when(me > 0)
    def _():
        state_copy.wait_recv()

    state = [enter_ref[v] for v in range(groups)]
    lane = lax.broadcasted_iota(jnp.int32, (SUB, LANES), 1)
    at_low = sub == 0
    at_high = sub == SUB - 1
    chunk_now = 0
    for start, stop in segments(width, reach, chunk_len):
        chunk = (start + reach) // chunk_len
        if chunk != chunk_now:
            state = [pltpu.roll(x, pitch, 1) for x in state]
            chunk_now = chunk
        radius = strain_ref[start // STRETCH]
        gate2 = jnp.full((SUB, LANES), jnp.where(radius >= 2, -BIG, BIG), jnp.float32)
        gate3 = jnp.full((SUB, LANES), jnp.where(radius >= 3, -BIG, BIG), jnp.float32)
        mine = lax.rem(lane + (LANES - side_pairs) + LANES - chunk * pitch, LANES) < rows

        def advance(j, x):
            wide = {v: x[v] for v in range(groups)}
            for k in range(1, 4):
                wide[-k] = jnp.where(at_low, BIG, pltpu.roll(x[groups - k], 1, 0))
                wide[groups - 1 + k] = jnp.where(at_high, BIG, pltpu.roll(x[k - 1], SUB - 1, 0))
            pair = {v: jnp.minimum(wide[v], wide[v + 1]) for v in range(-1, groups)}
            new = []
            for v in range(groups):
                near3 = jnp.minimum(pair[v - 1], pair[v])
                two = jnp.maximum(jnp.minimum(wide[v - 2], wide[v + 2]), gate2)
                three = jnp.maximum(jnp.minimum(wide[v - 3], wide[v + 3]), gate3)
                total = m_ref[0, j, v] + jnp.minimum(near3, jnp.minimum(two, three))
                if chunk == 0:
                    y_ref[j, v] = total
                else:
                    y_ref[j, v] = jnp.where(mine, total, y_ref[j, v])
                new.append(total)
            return new

        base = chunk * chunk_len - reach
        state = lax.fori_loop(start - base, stop - base, advance, state, unroll=stop - start)

    @pl.when(me < count - 1)
    def _():
        for v in range(groups):
            send_ref[v] = pltpu.roll(state[v], (LANES - chunk_now * pitch) % LANES, 1)
        state_copy.start()

    def least(j, carry):
        low = y_ref[j, 0]
        for v in range(1, groups):
            low = jnp.minimum(low, y_ref[j, v])
        low = jnp.min(low, axis=0, keepdims=True)
        low_ref[pl.ds(j, 1), :] = low
        return carry

    lax.fori_loop(0, chunk_len, least, 0, unroll=5)

    for lag in range(L):
        sub_index, v = lag // groups, lag % groups
        cells = y_ref[0:chunk_len, v, sub_index, :] - low_ref[0:chunk_len, :]
        flat = jnp.transpose(cells)
        flat = jnp.concatenate([flat, flat[0 : 2 * SUB]], axis=0)
        for e in range(classes):
            parts = []
            for c in range(chunks):
                begin = max(reach - c * chunk_len, 0)
                end = min(width + reach - c * chunk_len, chunk_len)
                if end > begin:
                    at = c * pitch + side_pairs + e * own
                    parts.append(flat[at : at + own, begin:end])
            out_ref[lag, pl.ds(e, own, stride=classes), :] = jnp.concatenate(parts, axis=1)

    @pl.when(me < count - 1)
    def _():
        state_copy.wait_send()

    for di, dj in OFFSETS:

        @pl.when(present(di, dj))
        def _():
            for copy in halo_copies(di, dj):
                copy.wait_send()


def per_device(near_trace, far_trace, inline_weight, time_weight, lag_low, lag_high, strain):
    rows, width = near_trace.shape
    reach = ITERS
    groups = L // SUB
    classes = 2
    own = rows // classes
    side_pairs = -(-reach // classes)
    pitch = -(-(rows + side_pairs) // 1)
    chunks = LANES // pitch
    chunk_len = -(-(width + 2 * reach) // chunks)
    count = lax.axis_size("tm")
    count_in = lax.axis_size("inline")

    mark = lax.broadcasted_iota(jnp.int32, (rows, width), 1)
    bounds = jnp.where(mark == 0, lag_low[:, None], lag_high[:, None])
    vmem = pl.BlockSpec(memory_space=pltpu.VMEM)
    dims = (
        rows,
        width,
        reach,
        classes,
        own,
        side_pairs,
        pitch,
        chunks,
        chunk_len,
        count,
        count_in,
    )
    whole = -(-chunk_len // SUB) * SUB
    deep = -(-(chunk_len + L) // SUB) * SUB
    return pl.pallas_call(
        functools.partial(kernel, dims),
        out_shape=jax.ShapeDtypeStruct((L, rows, width), jnp.float32),
        in_specs=[pl.BlockSpec(memory_space=pl.ANY)] * 5
        + [pl.BlockSpec(memory_space=pltpu.SMEM)],
        out_specs=vmem,
        scratch_shapes=[
            pltpu.VMEM((2, rows, width), jnp.float32),
            pltpu.VMEM((3, rows, width), jnp.int32),
            pltpu.VMEM((9, 2, rows, width), jnp.float32),
            pltpu.VMEM((9, 3, rows, width), jnp.int32),
            pltpu.VMEM((2, 3 * width, LANES), jnp.float32),
            pltpu.VMEM((classes, deep, LANES), jnp.float32),
            pltpu.VMEM((classes, whole, LANES), jnp.float32),
            pltpu.VMEM((2 * classes + 1, whole, LANES), jnp.float32),
            pltpu.VMEM((classes, chunk_len + 1, groups, SUB, LANES), jnp.float32),
            pltpu.VMEM((whole, groups, SUB, LANES), jnp.float32),
            pltpu.VMEM((whole, LANES), jnp.float32),
            pltpu.VMEM((groups, SUB, LANES), jnp.float32),
            pltpu.VMEM((groups, SUB, LANES), jnp.float32),
            pltpu.SemaphoreType.DMA((5,)),
            pltpu.SemaphoreType.DMA((2, 9)),
            pltpu.SemaphoreType.DMA((2, 9)),
            pltpu.SemaphoreType.DMA,
            pltpu.SemaphoreType.DMA,
        ],
        compiler_params=pltpu.CompilerParams(collective_id=0, has_side_effects=True),
    )(far_trace, near_trace, inline_weight, time_weight, bounds, strain)


def solution(mesh):
    return jax.shard_map(
        per_device,
        mesh=mesh,
        in_specs=(
            P(("group", "inline"), "tm"),
            P(("group", "inline"), "tm"),
            P(("group", "inline"), "tm"),
            P(("group", "inline"), "tm"),
            P(("group", "inline")),
            P(("group", "inline")),
            P(("group", "tm")),
        ),
        out_specs=P(None, ("group", "inline"), "tm"),
        check_vma=False,
    )
```
